32 devices in a mesh: row: 4 (over z), col: 8 (over y, x, core).
Axes of the slice: x: 2, y: 2, z: 4, core: 2. Of those that a mesh axis runs over, the one named last changes fastest.
Arguments:
- matrix: float32 [16384, 4096], P('row', 'col'), may hold values from -6 to 6
- leaf_v: float32 [2, 16384, 256], P(None, ('row', 'col')), may hold values from -0.09375 to 0.09375
- leaf_t: float32 [2, 1024, 256], P(None, 'row'), may hold values from -0.375 to 0.375
- tree_v: float32 [2, 3, 512, 256], replicated, may hold values from -0.25 to 0.25
- tree_t: float32 [2, 3, 256, 256], replicated, may hold values from -0.375 to 0.375
Outputs:
- updated: float32 [16384, 4096], P('row', 'col')
The draws below stay inside these ranges and needn't reach their ends.
All inputs are finite; a program needn't handle non-finite values.
Results may differ from the reference program's by a relative error of at most 0.0001.
Values sent between devices are 32-bit elements; how exact they have to be, the bound alone decides.
A program may use at most 128 MiB of HBM per device.

```python
import jax
import jax.numpy as jnp
from jax import lax

B = 256
PANELS = 2
ROWS_DEV = 4096
M = 16384
NC = 4096
N_ROW = 4


def steps_of(key, dims, shards, low, top_value):
    factor_of = 1.0
    for axis_at, parts in shards:
        steps = jax.random.uniform(jax.random.fold_in(jax.random.fold_in(key, 6), axis_at), (parts,), jnp.float32, low / len(shards), top_value / len(shards))
        factor_of = factor_of * jnp.repeat(jnp.exp(steps), dims[axis_at] // parts).reshape((-1,) + (1,) * (len(dims) - 1 - axis_at))
    return factor_of


def normal_values(stream_key, dims, spread, limit, pieces=(), kind=jnp.bfloat16):
    array = spread * jax.random.normal(stream_key, dims, jnp.float32)
    if pieces:
        array = array * steps_of(stream_key, dims, pieces, -0.22, 0.18)
    return jnp.clip(array, -limit, limit).astype(kind)


def setup_inputs(seed: int = 0) -> dict:
    key_of = jax.random.split(jax.random.key(seed), 6)
    return {
        "matrix": normal_values(key_of[0], (M, NC), 1.0, 6.0, ((0, 4), (1, 8)), jnp.float32),
        "leaf_v": normal_values(key_of[1], (PANELS, M, B), ROWS_DEV ** -0.5, 0.09375, ((1, 32),), jnp.float32),
        "leaf_t": normal_values(key_of[2], (PANELS, N_ROW * B, B), B ** -0.5, 0.375, ((1, 4),), jnp.float32),
        "tree_v": normal_values(key_of[3], (PANELS, N_ROW - 1, 2 * B, B), (2 * B) ** -0.5, 0.25, (), jnp.float32),
        "tree_t": normal_values(key_of[4], (PANELS, N_ROW - 1, B, B), B ** -0.5, 0.375, (), jnp.float32),
    }


def reference(matrix, leaf_v, leaf_t, tree_v, tree_t):
    highest = lax.Precision.HIGHEST
    blocks = matrix.reshape(N_ROW, ROWS_DEV, matrix.shape[1])
    for panel in range(PANELS):
        vectors = leaf_v[panel].reshape(N_ROW, ROWS_DEV, B)
        middle = leaf_t[panel].reshape(N_ROW, B, B)
        inner = jnp.einsum("rkb,rkn->rbn", vectors, blocks, precision=highest)
        scaled = jnp.einsum("rcb,rcn->rbn", middle, inner, precision=highest)
        blocks = blocks - jnp.einsum("rkb,rbn->rkn", vectors, scaled, precision=highest)
        tops = [blocks[index, :B] for index in range(N_ROW)]
        stride = 1
        level = 0
        while stride < N_ROW:
            for upper in range(0, N_ROW, 2 * stride):
                node = N_ROW - (N_ROW >> level) + upper // (2 * stride)
                pair_v = tree_v[panel, node]
                pair_t = tree_t[panel, node]
                inner = jnp.dot(pair_v[:B].T, tops[upper], precision=highest) + jnp.dot(pair_v[B:].T, tops[upper + stride], precision=highest)
                scaled = jnp.dot(pair_t.T, inner, precision=highest)
                tops[upper] = tops[upper] - jnp.dot(pair_v[:B], scaled, precision=highest)
                tops[upper + stride] = tops[upper + stride] - jnp.dot(pair_v[B:], scaled, precision=highest)
            stride = stride * 2
            level = level + 1
        blocks = jnp.concatenate([jnp.stack(tops), blocks[:, B:]], axis=1)
    return blocks.reshape(matrix.shape)
```

```python
import functools

import jax
import jax.numpy as jnp
from jax import lax
from jax.experimental import pallas as pl
from jax.experimental.pallas import tpu as pltpu
from jax.sharding import PartitionSpec as P

MESH = pl.DeviceIdType.MESH


def flip(index, mask):
    bit = 1
    while bit <= mask:
        if mask & bit:
            index = index + bit - 2 * bit * lax.rem(lax.div(index, bit), 2)
        bit *= 2
    return index


def halves(x):
    high = x.astype(jnp.bfloat16)
    return high, (x - high.astype(jnp.float32)).astype(jnp.bfloat16)


def product(left, right, dims):
    def one(a, b):
        return lax.dot_general(a, b, (dims, ((), ())), preferred_element_type=jnp.float32)

    (lh, ll), (rh, rl) = left, right
    return one(lh, rh) + (one(lh, rl) + one(ll, rh))


def left_product(left, right):
    return product(halves(left), halves(right), ((0,), (0,)))


def right_product(left, right):
    return product(halves(left), right, ((1,), (0,)))


def tile_of(rows, step, most):
    count = rows // step
    best = max(k for k in range(1, most // step + 1) if count % k == 0)
    return best * step


def kernel(grid_rows, chips, matrix, leaf_v, leaf_t, tree_v, tree_t, out,
           work, vectors, inner, scaled, top, other, pair_v, pair_t,
           load_sem, tree_sem, store_sem, send_sem, recv_sem, core_send, core_recv, top_send, top_recv):
    panels, own_rows, width = leaf_v.shape
    rows = work.shape[0]
    levels = grid_rows.bit_length() - 1
    bits = chips.bit_length() - 1
    half_rows = own_rows // 2
    unit = 2 * own_rows
    position = lax.axis_index("row")
    column = lax.axis_index("col")
    chip = lax.div(column, 2)
    core = lax.rem(column, 2)

    def device(which_chip, which_core):
        return {"row": position, "col": which_chip * 2 + which_core}

    def load_work(r):
        start = pl.ds(pl.multiple_of(flip(chip, r) * unit, unit), unit)
        return pltpu.make_async_copy(matrix.at[start], work.at[start], load_sem.at[panels + r])

    def load_own(p):
        start = pl.ds(pl.multiple_of(column * own_rows, own_rows), own_rows)
        return pltpu.make_async_copy(leaf_v.at[p], vectors.at[p, start], load_sem.at[p])

    def load_pair(p, level):
        node = grid_rows - (grid_rows >> level) + lax.div(position, 2 << level)
        return (pltpu.make_async_copy(tree_v.at[p, node], pair_v.at[p, level], tree_sem.at[p, level, 0]),
                pltpu.make_async_copy(tree_t.at[p, node], pair_t.at[p, level], tree_sem.at[p, level, 1]))

    load_own(0).start()
    for r in range(chips):
        load_work(r).start()
    for p in range(1, panels):
        load_own(p).start()
    for p in range(panels):
        for level in range(levels):
            for copy in load_pair(p, level):
                copy.start()

    barrier = pltpu.get_barrier_semaphore()
    partners = [device(chip, 1 - core)]
    partners += [device(flip(chip, 1 << b), core) for b in range(bits)]
    partners += [{"row": flip(position, 1 << level), "col": column} for level in range(levels)]
    for partner in partners:
        pl.semaphore_signal(barrier, inc=1, device_id=partner, device_id_type=MESH)
    pl.semaphore_wait(barrier, len(partners))

    orders = [list(range(bits)), list(reversed(range(bits)))]

    def piece(p, r, h, on_core):
        start = (flip(chip, r) * 2 + on_core) * own_rows + h * half_rows
        return vectors.at[p, pl.ds(pl.multiple_of(start, half_rows), half_rows)]

    def source(p, r, h):
        if r == 0:
            return leaf_v.at[p, pl.ds(h * half_rows, half_rows)]
        return piece(p, r, h, core)

    def chip_copy(p, r, h, bit):
        return pltpu.make_async_remote_copy(
            source(p, r, h), piece(p, r, h, core), send_sem.at[p, r, h, bit],
            recv_sem.at[p, r | 1 << bit, h], device_id=device(flip(chip, 1 << bit), core), device_id_type=MESH)

    def core_copy(p, r, h):
        return pltpu.make_async_remote_copy(
            source(p, r, h), piece(p, r, h, core), core_send.at[p, r, h],
            core_recv.at[p, r, h], device_id=device(chip, 1 - core), device_id_type=MESH)

    def core_arrival(p, r, h):
        there = piece(p, r, h, 1 - core)
        pltpu.make_async_remote_copy(
            there, there, core_send.at[p, r, h], core_recv.at[p, r, h],
            device_id=device(chip, 1 - core), device_id_type=MESH).wait_recv()

    def chip_arrival(p, r, h):
        here = piece(p, r, h, core)
        pltpu.make_async_remote_copy(
            here, here, core_send.at[p, r, h], recv_sem.at[p, r, h],
            device_id=device(chip, 1 - core), device_id_type=MESH).wait_recv()

    started = []

    def start(copy):
        copy.start()
        started.append(copy)

    def send_own(p):
        for k in range(bits):
            for h in range(2):
                start(chip_copy(p, 0, h, orders[h][k]))
        for h in range(2):
            start(core_copy(p, 0, h))

    events = []
    for s in range(bits):
        for h in range(2):
            before = orders[h][:s]
            for m in range(chips):
                if m & ~sum(1 << b for b in before) == 0:
                    events.append((s, bin(m).count("1"), m | 1 << orders[h][s], h))
    events.sort()

    def arrive(p, event):
        s, _, r, h = event
        chip_arrival(p, r, h)
        for bit in orders[h][s + 1:]:
            start(chip_copy(p, r, h, bit))
        start(core_copy(p, r, h))

    tile = tile_of(unit, min(unit, 256), 512)

    def accumulate(p, first, count):
        for r in range(first, first + count):
            for h in range(2):
                core_arrival(p, r, h)
            if p == 0:
                load_work(r).wait()
        if first == 0:
            load_own(p).wait()

        def step(i, carry):
            r = lax.div(i, unit // tile) + first
            at = chip
            for b in range(bits):
                set_bit = lax.rem(lax.div(r, 1 << b), 2)
                have = lax.rem(lax.div(chip, 1 << b), 2)
                at = at + (1 << b) * set_bit * (1 - 2 * have)
            start_row = pl.multiple_of(at * unit + lax.rem(i, unit // tile) * tile, tile)
            inner[...] += left_product(vectors[p, pl.ds(start_row, tile)], work[pl.ds(start_row, tile)])
            return carry

        lax.fori_loop(0, count * (unit // tile), step, 0)

    def make_scaled(p):
        found = left_product(leaf_t[p], inner[...])
        high, low = halves(found)
        scaled[0] = high
        scaled[1] = low
        inner[...] = jnp.zeros_like(inner)

    down = tile_of(rows - width, width, 768)

    def store_rows(i):
        span = pl.ds(pl.multiple_of(width + i * down, width), down)
        return pltpu.make_async_copy(work.at[span], out.at[span], store_sem.at[1])

    def subtract(p, last):
        def step(i, carry):
            span = pl.ds(pl.multiple_of(width + i * down, width), down)
            work[span] = work[span] - right_product(vectors[p, span], (scaled[0], scaled[1]))
            return carry

        lax.fori_loop(0, (rows - width) // down, step, 0)

    def top_copy(p, level):
        return pltpu.make_async_remote_copy(
            top, other.at[p, level], top_send.at[p, level], top_recv.at[p, level],
            device_id={"row": flip(position, 1 << level), "col": column}, device_id_type=MESH)

    def active(level):
        return lax.rem(position, 1 << level) == 0

    def send_top(p, level):
        @pl.when(active(level))
        def _():
            top_copy(p, level).start()

    def combine(p, level):
        for copy in load_pair(p, level):
            copy.wait()

        @pl.when(active(level))
        def _():
            lower = lax.rem(lax.div(position, 1 << level), 2)
            own = pair_v[p, level, pl.ds(pl.multiple_of(lower * width, width), width)]
            theirs = pair_v[p, level, pl.ds(pl.multiple_of((1 - lower) * width, width), width)]
            inside = left_product(own, top[...])
            copy = top_copy(p, level)
            copy.wait_recv()
            inside = inside + left_product(theirs, other[p, level])
            weight = left_product(pair_t[p, level], inside)
            change = right_product(own, halves(weight))
            copy.wait_send()
            top[...] = top[...] - change

    inner[...] = jnp.zeros_like(inner)
    send_own(0)
    accumulate(0, 0, 1)
    early, late = events[:-2], events[-2:]
    for event in early:
        arrive(0, event)
    if panels > 1:
        send_own(1)
    accumulate(0, 1, chips - 2)
    for event in late:
        arrive(0, event)
    accumulate(0, chips - 1, 1)
    make_scaled(0)
    for p in range(panels):
        if p == 0:
            before_top = work[:width]
        else:
            before_top = top[...]
        top[...] = before_top - right_product(vectors[p, :width], (scaled[0], scaled[1]))
        send_top(p, 0)
        subtract(p, p == panels - 1)
        if p == panels - 1:
            span = pl.ds(width, rows - width)
            rest = pltpu.make_async_copy(work.at[span], out.at[span], store_sem.at[1])
            rest.start()
            for level in range(levels):
                combine(p, level)
                if level + 1 < levels:
                    send_top(p, level + 1)
            last = pltpu.make_async_copy(top, out.at[pl.ds(0, width)], store_sem.at[0])
            last.start()
            last.wait()
            rest.wait()
            break
        q = p + 1
        work[:width] = jnp.zeros((width, work.shape[1]), jnp.float32)
        first = len(events) - 4
        for event in events[:first]:
            arrive(q, event)
        accumulate(q, 0, 1)
        for event in events[first:-2]:
            arrive(q, event)
        if q + 1 < panels:
            send_own(q + 1)
        combine(p, 0)
        if levels > 1:
            send_top(p, 1)
        accumulate(q, 1, chips - 2)
        for event in late:
            arrive(q, event)
        accumulate(q, chips - 1, 1)
        for level in range(1, levels):
            combine(p, level)
            if level + 1 < levels:
                send_top(p, level + 1)
        inner[...] += left_product(vectors[q, :width], top[...])
        make_scaled(q)
    for copy in started:
        copy.wait_send()


def solution(mesh):
    grid_rows = mesh.shape["row"]
    chips = mesh.shape["col"] // 2
    levels = grid_rows.bit_length() - 1
    bits = chips.bit_length() - 1

    def local(matrix, leaf_v, leaf_t, tree_v, tree_t):
        rows, columns = matrix.shape
        panels, _, width = leaf_v.shape
        f32, dma = jnp.float32, pltpu.SemaphoreType.DMA
        hbm = pl.BlockSpec(memory_space=pl.ANY)
        vmem = pl.BlockSpec(memory_space=pltpu.VMEM)
        return pl.pallas_call(
            functools.partial(kernel, grid_rows, chips),
            out_shape=jax.ShapeDtypeStruct(matrix.shape, f32),
            in_specs=[hbm, hbm, vmem, hbm, hbm],
            out_specs=hbm,
            scratch_shapes=[
                pltpu.VMEM((rows, columns), f32),
                pltpu.VMEM((panels, rows, width), f32),
                pltpu.VMEM((width, columns), f32),
                pltpu.VMEM((2, width, columns), jnp.bfloat16),
                pltpu.VMEM((width, columns), f32),
                pltpu.VMEM((panels, levels, width, columns), f32),
                pltpu.VMEM((panels, levels, 2 * width, width), f32),
                pltpu.VMEM((panels, levels, width, width), f32),
                dma((panels + chips,)),
                dma((panels, levels, 2)),
                dma((2,)),
                dma((panels, chips, 2, bits)),
                dma((panels, chips, 2)),
                dma((panels, chips, 2)),
                dma((panels, chips, 2)),
                dma((panels, levels)),
                dma((panels, levels)),
            ],
            compiler_params=pltpu.CompilerParams(
                collective_id=0, has_side_effects=True, vmem_limit_bytes=56 * 1024 * 1024
            ),
        )(matrix, leaf_v, leaf_t, tree_v, tree_t)

    placed = (P("row", "col"), P(None, ("row", "col"), None), P(None, "row", None), P(), P())
    return jax.shard_map(local, mesh=mesh, in_specs=placed, out_specs=P("row", "col"), check_vma=False)
```

```python
import functools

import jax
import jax.numpy as jnp
from jax import lax
from jax.experimental import pallas as pl
from jax.experimental.pallas import tpu as pltpu
from jax.sharding import PartitionSpec as P

MESH = pl.DeviceIdType.MESH


def flip(index, mask):
    bit = 1
    while bit <= mask:
        if mask & bit:
            index = index + bit - 2 * bit * lax.rem(lax.div(index, bit), 2)
        bit *= 2
    return index


def halves(x):
    high = x.astype(jnp.bfloat16)
    return high, (x - high.astype(jnp.float32)).astype(jnp.bfloat16)


def product(left, right, dims):
    def one(a, b):
        return lax.dot_general(a, b, (dims, ((), ())), preferred_element_type=jnp.float32)

    (lh, ll), (rh, rl) = left, right
    return one(lh, rh) + (one(lh, rl) + one(ll, rh))


def left_product(left, right):
    return product(halves(left), halves(right), ((0,), (0,)))


def right_product(left, right):
    return product(halves(left), right, ((1,), (0,)))


def tile_of(rows, step, most):
    count = rows // step
    best = max(k for k in range(1, most // step + 1) if count % k == 0)
    return best * step


def kernel(grid_rows, chips, matrix, leaf_v, leaf_t, tree_v, tree_t, out,
           work, vectors, inner, scaled, top, hub, other, pair_v, pair_t,
           load_sem, tree_sem, store_sem, send_sem, recv_sem, core_send, core_recv, top_send, top_recv):
    panels, own_rows, width = leaf_v.shape
    rows = work.shape[0]
    levels = grid_rows.bit_length() - 1
    bits = chips.bit_length() - 1
    half_rows = own_rows // 2
    unit = 2 * own_rows
    position = lax.axis_index("row")
    column = lax.axis_index("col")
    chip = lax.div(column, 2)
    core = lax.rem(column, 2)

    def device(which_chip, which_core):
        return {"row": position, "col": which_chip * 2 + which_core}

    def load_work(r):
        start = pl.ds(pl.multiple_of(flip(chip, r) * unit, unit), unit)
        return pltpu.make_async_copy(matrix.at[start], work.at[start], load_sem.at[panels + r])

    def load_own(p):
        start = pl.ds(pl.multiple_of(column * own_rows, own_rows), own_rows)
        return pltpu.make_async_copy(leaf_v.at[p], vectors.at[p, start], load_sem.at[p])

    def load_pair(p, level):
        node = grid_rows - (grid_rows >> level) + lax.div(position, 2 << level)
        return (pltpu.make_async_copy(tree_v.at[p, node], pair_v.at[p, level], tree_sem.at[p, level, 0]),
                pltpu.make_async_copy(tree_t.at[p, node], pair_t.at[p, level], tree_sem.at[p, level, 1]))

    load_own(0).start()
    for r in range(chips):
        load_work(r).start()
    for p in range(1, panels):
        load_own(p).start()
    for p in range(panels):
        for level in range(levels):
            for copy in load_pair(p, level):
                copy.start()

    barrier = pltpu.get_barrier_semaphore()
    partners = [device(chip, 1 - core)]
    partners += [device(flip(chip, 1 << b), core) for b in range(bits)]
    sideways = {"row": flip(position, 1), "col": column}
    across = {"row": grid_rows - 1 - position, "col": column}
    partners += [sideways, across]
    for partner in partners:
        pl.semaphore_signal(barrier, inc=1, device_id=partner, device_id_type=MESH)
    pl.semaphore_wait(barrier, len(partners))

    orders = [list(range(bits)), list(reversed(range(bits)))]

    def piece(p, r, h, on_core):
        start = (flip(chip, r) * 2 + on_core) * own_rows + h * half_rows
        return vectors.at[p, pl.ds(pl.multiple_of(start, half_rows), half_rows)]

    def source(p, r, h):
        if r == 0:
            return leaf_v.at[p, pl.ds(h * half_rows, half_rows)]
        return piece(p, r, h, core)

    def chip_copy(p, r, h, bit):
        return pltpu.make_async_remote_copy(
            source(p, r, h), piece(p, r, h, core), send_sem.at[p, r, h, bit],
            recv_sem.at[p, r | 1 << bit, h], device_id=device(flip(chip, 1 << bit), core), device_id_type=MESH)

    def core_copy(p, r, h):
        return pltpu.make_async_remote_copy(
            source(p, r, h), piece(p, r, h, core), core_send.at[p, r, h],
            core_recv.at[p, r, h], device_id=device(chip, 1 - core), device_id_type=MESH)

    def core_arrival(p, r, h):
        there = piece(p, r, h, 1 - core)
        pltpu.make_async_remote_copy(
            there, there, core_send.at[p, r, h], core_recv.at[p, r, h],
            device_id=device(chip, 1 - core), device_id_type=MESH).wait_recv()

    def chip_arrival(p, r, h):
        here = piece(p, r, h, core)
        pltpu.make_async_remote_copy(
            here, here, core_send.at[p, r, h], recv_sem.at[p, r, h],
            device_id=device(chip, 1 - core), device_id_type=MESH).wait_recv()

    started = []

    def start(copy):
        copy.start()
        started.append(copy)

    def send_own(p):
        for k in range(bits):
            for h in range(2):
                start(chip_copy(p, 0, h, orders[h][k]))
        for h in range(2):
            start(core_copy(p, 0, h))

    events = []
    for s in range(bits):
        for h in range(2):
            before = orders[h][:s]
            for m in range(chips):
                if m & ~sum(1 << b for b in before) == 0:
                    events.append((s, bin(m).count("1"), m | 1 << orders[h][s], h))
    events.sort()

    def arrive(p, event):
        s, _, r, h = event
        chip_arrival(p, r, h)
        for bit in orders[h][s + 1:]:
            start(chip_copy(p, r, h, bit))
        start(core_copy(p, r, h))

    tile = tile_of(unit, min(unit, 256), 512)

    def accumulate(p, first, count):
        for r in range(first, first + count):
            for h in range(2):
                core_arrival(p, r, h)
            if p == 0:
                load_work(r).wait()
        if first == 0:
            load_own(p).wait()

        def step(i, carry):
            r = lax.div(i, unit // tile) + first
            at = chip
            for b in range(bits):
                set_bit = lax.rem(lax.div(r, 1 << b), 2)
                have = lax.rem(lax.div(chip, 1 << b), 2)
                at = at + (1 << b) * set_bit * (1 - 2 * have)
            start_row = pl.multiple_of(at * unit + lax.rem(i, unit // tile) * tile, tile)
            inner[...] += left_product(vectors[p, pl.ds(start_row, tile)], work[pl.ds(start_row, tile)])
            return carry

        lax.fori_loop(0, count * (unit // tile), step, 0)

    down = tile_of(rows - width, width, 768)

    def subtract(p):
        def step(i, carry):
            span = pl.ds(pl.multiple_of(width + i * down, width), down)
            work[span] = work[span] - right_product(vectors[p, span], (scaled[0], scaled[1]))
            return carry

        lax.fori_loop(0, (rows - width) // down, step, 0)

    chunks, _, part = top.shape
    low, middle_low, middle_high = position == 0, position == 1, position == 2
    middle = jnp.logical_or(middle_low, middle_high)

    def exchange(buffer, p, j, stage, target):
        return pltpu.make_async_remote_copy(
            buffer, other.at[p, j, stage], top_send.at[p, j, stage], top_recv.at[p, j, stage],
            device_id=target, device_id_type=MESH)

    def head(p, j):
        columns = slice(j * part, (j + 1) * part)
        before = work[:width, columns] if p == 0 else top[j]
        inside = inner[:, columns]
        if p > 0:
            inside = inside + left_product(vectors[p, :width], before)
        weight = halves(left_product(leaf_t[p], inside))
        scaled[0, :, columns], scaled[1, :, columns] = weight
        top[j] = before - right_product(vectors[p, :width], weight)

        @pl.when(jnp.logical_not(middle_low))
        def _():
            exchange(top.at[j], p, j, 0, sideways).start()

    def first_level(p, j):
        if j == 0:
            for level in range(levels):
                for copy in load_pair(p, level):
                    copy.wait()

        @pl.when(jnp.logical_not(low))
        def _():
            lower = lax.rem(position, 2)
            own = pair_v[p, 0, pl.ds(pl.multiple_of(lower * width, width), width)]
            theirs = pair_v[p, 0, pl.ds(pl.multiple_of((1 - lower) * width, width), width)]
            inside = left_product(own, top[j])
            exchange(top.at[j], p, j, 0, sideways).wait_recv()
            inside = inside + left_product(theirs, other[p, j, 0])
            weight = halves(left_product(pair_t[p, 0], inside))

            @pl.when(middle_low)
            def _():
                hub[p, j] = other[p, j, 0] - right_product(theirs, weight)
                exchange(hub.at[p, j], p, j, 1, across).start()
                top[j] = top[j] - right_product(own, weight)

            @pl.when(jnp.logical_not(middle_low))
            def _():
                change = right_product(own, weight)
                exchange(top.at[j], p, j, 0, sideways).wait_send()
                top[j] = top[j] - change

            @pl.when(middle_high)
            def _():
                exchange(top.at[j], p, j, 1, across).start()

    def second_level(p, j):
        def update(buffer, half):
            own = pair_v[p, 1, half * width:(half + 1) * width]
            theirs = pair_v[p, 1, (1 - half) * width:(2 - half) * width]
            inside = left_product(own, buffer[...])
            copy = exchange(buffer, p, j, 1, across)
            copy.wait_recv()
            inside = inside + left_product(theirs, other[p, j, 1])
            weight = halves(left_product(pair_t[p, 1], inside))
            change = right_product(own, weight)
            copy.wait_send()
            buffer[...] = buffer[...] - change

        @pl.when(middle_low)
        def _():
            update(hub.at[p, j], 0)
            exchange(hub.at[p, j], p, j, 2, sideways).start()

        @pl.when(middle_high)
        def _():
            update(top.at[j], 1)

    def finish(p, j):
        @pl.when(low)
        def _():
            exchange(top.at[j], p, j, 0, sideways).wait_send()
            exchange(hub.at[p, j], p, j, 2, sideways).wait_recv()
            top[j] = other[p, j, 2]

    stage_one, stage_two, late = events[:-4], events[-4:-2], events[-2:]
    inner[...] = jnp.zeros_like(inner)
    send_own(0)
    accumulate(0, 0, 1)
    for event in stage_one + stage_two:
        arrive(0, event)
    if panels > 1:
        send_own(1)
    accumulate(0, 1, chips - 2)
    for event in late:
        arrive(0, event)
    accumulate(0, chips - 1, 1)
    for j in range(chunks):
        head(0, j)
    for p in range(panels):
        q = p + 1
        if q == panels:
            first_level(p, 0)
            first_level(p, 1)
            for j in range(2, chunks):
                first_level(p, j)
            subtract(p)
            span = pl.ds(width, rows - width)
            rest = pltpu.make_async_copy(work.at[span], out.at[span], store_sem.at[chunks])
            rest.start()
            for j in range(chunks):
                second_level(p, j)
            last = []
            for j in range(chunks):
                finish(p, j)
                copy = pltpu.make_async_copy(
                    top.at[j], out.at[pl.ds(0, width), pl.ds(j * part, part)], store_sem.at[j])
                copy.start()
                last.append(copy)
            for copy in last:
                copy.wait()
            rest.wait()
            break
        subtract(p)
        work[:width] = jnp.zeros((width, work.shape[1]), jnp.float32)
        inner[...] = jnp.zeros_like(inner)
        todo = [functools.partial(arrive, q, event) for event in stage_one]
        todo += [functools.partial(first_level, p, j) for j in range(2)]
        todo += [functools.partial(accumulate, q, 0, 1)]
        todo += [functools.partial(arrive, q, event) for event in stage_two]
        if q + 1 < panels:
            todo += [functools.partial(send_own, q + 1)]
        todo += [functools.partial(first_level, p, 2), functools.partial(second_level, p, 0)]
        todo += [functools.partial(accumulate, q, 1, chips - 2)]
        todo += [functools.partial(first_level, p, 3), functools.partial(second_level, p, 1)]
        todo += [functools.partial(arrive, q, event) for event in late]
        todo += [functools.partial(second_level, p, 2), functools.partial(accumulate, q, chips - 1, 1)]
        todo += [functools.partial(second_level, p, 3)]
        for step in todo:
            step()
        for j in range(chunks):
            finish(p, j)
            head(q, j)
    for p in range(panels):
        for j in range(chunks):
            @pl.when(middle_low)
            def _(p=p, j=j):
                exchange(hub.at[p, j], p, j, 2, sideways).wait_send()
    for copy in started:
        copy.wait_send()


def solution(mesh):
    grid_rows = mesh.shape["row"]
    chips = mesh.shape["col"] // 2
    levels = grid_rows.bit_length() - 1
    bits = chips.bit_length() - 1

    def local(matrix, leaf_v, leaf_t, tree_v, tree_t):
        rows, columns = matrix.shape
        chunks = 4
        part = columns // chunks
        panels, _, width = leaf_v.shape
        f32, dma = jnp.float32, pltpu.SemaphoreType.DMA
        hbm = pl.BlockSpec(memory_space=pl.ANY)
        vmem = pl.BlockSpec(memory_space=pltpu.VMEM)
        return pl.pallas_call(
            functools.partial(kernel, grid_rows, chips),
            out_shape=jax.ShapeDtypeStruct(matrix.shape, f32),
            in_specs=[hbm, hbm, vmem, hbm, hbm],
            out_specs=hbm,
            scratch_shapes=[
                pltpu.VMEM((rows, columns), f32),
                pltpu.VMEM((panels, rows, width), f32),
                pltpu.VMEM((width, columns), f32),
                pltpu.VMEM((2, width, columns), jnp.bfloat16),
                pltpu.VMEM((chunks, width, part), f32),
                pltpu.VMEM((panels, chunks, width, part), f32),
                pltpu.VMEM((panels, chunks, 3, width, part), f32),
                pltpu.VMEM((panels, levels, 2 * width, width), f32),
                pltpu.VMEM((panels, levels, width, width), f32),
                dma((panels + chips,)),
                dma((panels, levels, 2)),
                dma((chunks + 1,)),
                dma((panels, chips, 2, bits)),
                dma((panels, chips, 2)),
                dma((panels, chips, 2)),
                dma((panels, chips, 2)),
                dma((panels, chunks, 3)),
                dma((panels, chunks, 3)),
            ],
            compiler_params=pltpu.CompilerParams(
                collective_id=0, has_side_effects=True, vmem_limit_bytes=56 * 1024 * 1024
            ),
        )(matrix, leaf_v, leaf_t, tree_v, tree_t)

    placed = (P("row", "col"), P(None, ("row", "col"), None), P(None, "row", None), P(), P())
    return jax.shard_map(local, mesh=mesh, in_specs=placed, out_specs=P("row", "col"), check_vma=False)
```

```python
import functools

import jax
import jax.numpy as jnp
from jax import lax
from jax.experimental import pallas as pl
from jax.experimental.pallas import tpu as pltpu
from jax.sharding import PartitionSpec as P

MESH = pl.DeviceIdType.MESH


def flip(index, mask):
    bit = 1
    while bit <= mask:
        if mask & bit:
            index = index + bit - 2 * bit * lax.rem(lax.div(index, bit), 2)
        bit *= 2
    return index


def halves(x):
    high = x.astype(jnp.bfloat16)
    return high, (x - high.astype(jnp.float32)).astype(jnp.bfloat16)


def product(left, right, dims):
    def one(a, b):
        return lax.dot_general(a, b, (dims, ((), ())), preferred_element_type=jnp.float32)

    (lh, ll), (rh, rl) = left, right
    return one(lh, rh) + (one(lh, rl) + one(ll, rh))


def left_product(left, right):
    return product(halves(left), halves(right), ((0,), (0,)))


def right_product(left, right):
    return product(halves(left), right, ((1,), (0,)))


def tile_of(rows, step, most):
    count = rows // step
    best = max(k for k in range(1, most // step + 1) if count % k == 0)
    return best * step


def kernel(grid_rows, chips, matrix, leaf_v, leaf_t, tree_v, tree_t, out,
           work, vectors, inner, scaled, top, hub, other, pair_v, pair_t, node_map,
           load_sem, tree_sem, store_sem, send_sem, recv_sem, core_send, core_recv, top_send, top_recv):
    panels, own_rows, width = leaf_v.shape
    rows = work.shape[0]
    levels = grid_rows.bit_length() - 1
    bits = chips.bit_length() - 1
    half_rows = own_rows // 2
    unit = 2 * own_rows
    position = lax.axis_index("row")
    column = lax.axis_index("col")
    chip = lax.div(column, 2)
    core = lax.rem(column, 2)

    def device(which_chip, which_core):
        return {"row": position, "col": which_chip * 2 + which_core}

    def load_work(r):
        start = pl.ds(pl.multiple_of(flip(chip, r) * unit, unit), unit)
        return pltpu.make_async_copy(matrix.at[start], work.at[start], load_sem.at[panels + r])

    def load_own(p):
        start = pl.ds(pl.multiple_of(column * own_rows, own_rows), own_rows)
        return pltpu.make_async_copy(leaf_v.at[p], vectors.at[p, start], load_sem.at[p])

    def load_pair(p, level):
        node = grid_rows - (grid_rows >> level) + lax.div(position, 2 << level)
        return (pltpu.make_async_copy(tree_v.at[p, node], pair_v.at[p, level], tree_sem.at[p, level, 0]),
                pltpu.make_async_copy(tree_t.at[p, node], pair_t.at[p, level], tree_sem.at[p, level, 1]))

    load_own(0).start()
    for r in range(chips):
        load_work(r).start()
    for p in range(1, panels):
        load_own(p).start()
    for p in range(panels):
        for level in range(levels):
            for copy in load_pair(p, level):
                copy.start()

    barrier = pltpu.get_barrier_semaphore()
    partners = [device(chip, 1 - core)]
    partners += [device(flip(chip, 1 << b), core) for b in range(bits)]
    sideways = {"row": flip(position, 1), "col": column}
    across = {"row": grid_rows - 1 - position, "col": column}
    partners += [sideways, across]
    for partner in partners:
        pl.semaphore_signal(barrier, inc=1, device_id=partner, device_id_type=MESH)
    pl.semaphore_wait(barrier, len(partners))

    orders = [list(range(bits)), list(reversed(range(bits)))]

    def piece(p, r, h, on_core):
        start = (flip(chip, r) * 2 + on_core) * own_rows + h * half_rows
        return vectors.at[p, pl.ds(pl.multiple_of(start, half_rows), half_rows)]

    def source(p, r, h):
        if r == 0:
            return leaf_v.at[p, pl.ds(h * half_rows, half_rows)]
        return piece(p, r, h, core)

    def chip_copy(p, r, h, bit):
        return pltpu.make_async_remote_copy(
            source(p, r, h), piece(p, r, h, core), send_sem.at[p, r, h, bit],
            recv_sem.at[p, r | 1 << bit, h], device_id=device(flip(chip, 1 << bit), core), device_id_type=MESH)

    def core_copy(p, r, h):
        return pltpu.make_async_remote_copy(
            source(p, r, h), piece(p, r, h, core), core_send.at[p, r, h],
            core_recv.at[p, r, h], device_id=device(chip, 1 - core), device_id_type=MESH)

    def core_arrival(p, r, h):
        there = piece(p, r, h, 1 - core)
        pltpu.make_async_remote_copy(
            there, there, core_send.at[p, r, h], core_recv.at[p, r, h],
            device_id=device(chip, 1 - core), device_id_type=MESH).wait_recv()

    def chip_arrival(p, r, h):
        here = piece(p, r, h, core)
        pltpu.make_async_remote_copy(
            here, here, core_send.at[p, r, h], recv_sem.at[p, r, h],
            device_id=device(chip, 1 - core), device_id_type=MESH).wait_recv()

    started = []

    def start(copy):
        copy.start()
        started.append(copy)

    def send_own(p):
        for k in range(bits):
            for h in range(2):
                start(chip_copy(p, 0, h, orders[h][k]))
        for h in range(2):
            start(core_copy(p, 0, h))

    events = []
    for s in range(bits):
        for h in range(2):
            before = orders[h][:s]
            for m in range(chips):
                if m & ~sum(1 << b for b in before) == 0:
                    events.append((s, bin(m).count("1"), m | 1 << orders[h][s], h))
    events.sort()

    def arrive(p, event):
        s, _, r, h = event
        chip_arrival(p, r, h)
        for bit in orders[h][s + 1:]:
            start(chip_copy(p, r, h, bit))
        start(core_copy(p, r, h))

    tile = tile_of(unit, min(unit, 256), 512)

    def accumulate(p, first, count):
        for r in range(first, first + count):
            for h in range(2):
                core_arrival(p, r, h)
            if p == 0:
                load_work(r).wait()
        if first == 0:
            load_own(p).wait()

        def step(i, carry):
            r = lax.div(i, unit // tile) + first
            at = chip
            for b in range(bits):
                set_bit = lax.rem(lax.div(r, 1 << b), 2)
                have = lax.rem(lax.div(chip, 1 << b), 2)
                at = at + (1 << b) * set_bit * (1 - 2 * have)
            start_row = pl.multiple_of(at * unit + lax.rem(i, unit // tile) * tile, tile)
            inner[...] += left_product(vectors[p, pl.ds(start_row, tile)], work[pl.ds(start_row, tile)])
            return carry

        lax.fori_loop(0, count * (unit // tile), step, 0)

    down = tile_of(rows - width, width, 768)

    downs = (rows - width) // down

    def subtract(p, first, last):
        def step(i, carry):
            span = pl.ds(pl.multiple_of(width + i * down, width), down)
            work[span] = work[span] - right_product(vectors[p, span], (scaled[0], scaled[1]))
            return carry

        lax.fori_loop(first, last, step, 0)

    chunks, _, part = top.shape
    low, middle_low, middle_high = position == 0, position == 1, position == 2
    middle = jnp.logical_or(middle_low, middle_high)

    def exchange(buffer, p, j, stage, target):
        return pltpu.make_async_remote_copy(
            buffer, other.at[p, j, stage], top_send.at[p, j, stage], top_recv.at[p, j, stage],
            device_id=target, device_id_type=MESH)

    def prepare(p):
        for level in range(levels):
            for copy in load_pair(p, level):
                copy.wait()
            pair = halves(pair_v[p, level])
            weight = product(halves(pair_t[p, level]), pair, ((0,), (1,)))
            whole = right_product(pair_v[p, level], halves(weight))
            node_map[p, level, 0], node_map[p, level, 1] = halves(whole)

    def mapped(p, level, to, count, source, value):
        block = (pl.ds(to, count), pl.ds(source, width))
        return product((node_map[(p, level, 0) + block], node_map[(p, level, 1) + block]), halves(value), ((1,), (0,)))

    def head(p):
        inside = inner[...]
        if p > 0:
            inside = inside + left_product(vectors[p, :width], jnp.concatenate([top[j] for j in range(chunks)], axis=1))
        weight = halves(left_product(leaf_t[p], inside))
        scaled[0], scaled[1] = weight
        above = halves(vectors[p, :width])
        for j in range(chunks):
            columns = slice(j * part, (j + 1) * part)
            before = work[:width, columns] if p == 0 else top[j]
            top[j] = before - product(above, (weight[0][:, columns], weight[1][:, columns]), ((1,), (0,)))

            @pl.when(jnp.logical_not(middle_low))
            def _(j=j):
                exchange(top.at[j], p, j, 0, sideways).start()

    def first_level(p, j):
        @pl.when(middle_low)
        def _():
            change = mapped(p, 0, 0, 2 * width, width, top[j])
            exchange(top.at[j], p, j, 0, sideways).wait_recv()
            theirs = other[p, j, 0]
            change = change + mapped(p, 0, 0, 2 * width, 0, theirs)
            hub[p, j] = theirs - change[:width]
            exchange(hub.at[p, j], p, j, 1, across).start()
            top[j] = top[j] - change[width:]

        @pl.when(position > 1)
        def _():
            mine = pl.multiple_of(lax.rem(position, 2) * width, width)
            theirs = pl.multiple_of(width - lax.rem(position, 2) * width, width)
            change = mapped(p, 0, mine, width, mine, top[j])
            copy = exchange(top.at[j], p, j, 0, sideways)
            copy.wait_recv()
            change = change + mapped(p, 0, mine, width, theirs, other[p, j, 0])
            copy.wait_send()
            top[j] = top[j] - change

            @pl.when(middle_high)
            def _():
                exchange(top.at[j], p, j, 1, across).start()

    def second_level(p, j):
        def update(buffer, half):
            mine, theirs = half * width, (1 - half) * width
            change = mapped(p, 1, mine, width, mine, buffer[...])
            copy = exchange(buffer, p, j, 1, across)
            copy.wait_recv()
            change = change + mapped(p, 1, mine, width, theirs, other[p, j, 1])
            copy.wait_send()
            buffer[...] = buffer[...] - change

        @pl.when(middle_low)
        def _():
            update(hub.at[p, j], 0)
            exchange(hub.at[p, j], p, j, 2, sideways).start()

        @pl.when(middle_high)
        def _():
            update(top.at[j], 1)

    def finish(p, j):
        @pl.when(low)
        def _():
            exchange(top.at[j], p, j, 0, sideways).wait_send()
            exchange(hub.at[p, j], p, j, 2, sideways).wait_recv()
            top[j] = other[p, j, 2]

    stage_one, stage_two, late = events[:-4], events[-4:-2], events[-2:]
    inner[...] = jnp.zeros_like(inner)
    send_own(0)
    accumulate(0, 0, 1)
    for p in range(panels):
        prepare(p)
    for event in stage_one + stage_two:
        arrive(0, event)
    if panels > 1:
        send_own(1)
    accumulate(0, 1, chips - 2)
    for event in late:
        arrive(0, event)
    accumulate(0, chips - 1, 1)
    head(0)
    for p in range(panels):
        q = p + 1
        if q == panels:
            subtract(p, 0, downs // 2 + 1)
            first_level(p, 0)
            first_level(p, 1)
            subtract(p, downs // 2 + 1, downs)
            span = pl.ds(width, rows - width)
            rest = pltpu.make_async_copy(work.at[span], out.at[span], store_sem.at[chunks])
            rest.start()
            for j in range(2, chunks):
                second_level(p, j - 2)
                first_level(p, j)
            for j in range(chunks - 2, chunks):
                second_level(p, j)
            last = []
            for j in range(chunks):
                finish(p, j)
                copy = pltpu.make_async_copy(
                    top.at[j], out.at[pl.ds(0, width), pl.ds(j * part, part)], store_sem.at[j])
                copy.start()
                last.append(copy)
            for copy in last:
                copy.wait()
            rest.wait()
            break
        subtract(p, 0, downs)
        work[:width] = jnp.zeros((width, work.shape[1]), jnp.float32)
        inner[...] = jnp.zeros_like(inner)
        todo = [functools.partial(arrive, q, event) for event in stage_one]
        todo += [functools.partial(first_level, p, j) for j in range(2)]
        todo += [functools.partial(accumulate, q, 0, 1)]
        todo += [functools.partial(arrive, q, event) for event in stage_two]
        if q + 1 < panels:
            todo += [functools.partial(send_own, q + 1)]
        todo += [functools.partial(first_level, p, 2), functools.partial(second_level, p, 0)]
        todo += [functools.partial(accumulate, q, 1, chips - 2)]
        todo += [functools.partial(first_level, p, 3), functools.partial(second_level, p, 1)]
        todo += [functools.partial(arrive, q, event) for event in late]
        todo += [functools.partial(second_level, p, 2), functools.partial(accumulate, q, chips - 1, 1)]
        todo += [functools.partial(second_level, p, 3)]
        for step in todo:
            step()
        for j in range(chunks):
            finish(p, j)
        head(q)
    for p in range(panels):
        for j in range(chunks):
            @pl.when(middle_low)
            def _(p=p, j=j):
                exchange(hub.at[p, j], p, j, 2, sideways).wait_send()
    for copy in started:
        copy.wait_send()


def solution(mesh):
    grid_rows = mesh.shape["row"]
    chips = mesh.shape["col"] // 2
    levels = grid_rows.bit_length() - 1
    bits = chips.bit_length() - 1

    def local(matrix, leaf_v, leaf_t, tree_v, tree_t):
        rows, columns = matrix.shape
        chunks = 4
        part = columns // chunks
        panels, _, width = leaf_v.shape
        f32, dma = jnp.float32, pltpu.SemaphoreType.DMA
        hbm = pl.BlockSpec(memory_space=pl.ANY)
        vmem = pl.BlockSpec(memory_space=pltpu.VMEM)
        return pl.pallas_call(
            functools.partial(kernel, grid_rows, chips),
            out_shape=jax.ShapeDtypeStruct(matrix.shape, f32),
            in_specs=[hbm, hbm, vmem, hbm, hbm],
            out_specs=hbm,
            scratch_shapes=[
                pltpu.VMEM((rows, columns), f32),
                pltpu.VMEM((panels, rows, width), f32),
                pltpu.VMEM((width, columns), f32),
                pltpu.VMEM((2, width, columns), jnp.bfloat16),
                pltpu.VMEM((chunks, width, part), f32),
                pltpu.VMEM((panels, chunks, width, part), f32),
                pltpu.VMEM((panels, chunks, 3, width, part), f32),
                pltpu.VMEM((panels, levels, 2 * width, width), f32),
                pltpu.VMEM((panels, levels, width, width), f32),
                pltpu.VMEM((panels, levels, 2, 2 * width, 2 * width), jnp.bfloat16),
                dma((panels + chips,)),
                dma((panels, levels, 2)),
                dma((chunks + 1,)),
                dma((panels, chips, 2, bits)),
                dma((panels, chips, 2)),
                dma((panels, chips, 2)),
                dma((panels, chips, 2)),
                dma((panels, chunks, 3)),
                dma((panels, chunks, 3)),
            ],
            compiler_params=pltpu.CompilerParams(
                collective_id=0, has_side_effects=True, vmem_limit_bytes=56 * 1024 * 1024
            ),
        )(matrix, leaf_v, leaf_t, tree_v, tree_t)

    placed = (P("row", "col"), P(None, ("row", "col"), None), P(None, "row", None), P(), P())
    return jax.shard_map(local, mesh=mesh, in_specs=placed, out_specs=P("row", "col"), check_vma=False)
```

```python
import functools

import jax
import jax.numpy as jnp
from jax import lax
from jax.experimental import pallas as pl
from jax.experimental.pallas import tpu as pltpu
from jax.sharding import PartitionSpec as P

MESH = pl.DeviceIdType.MESH


def flip(index, mask):
    bit = 1
    while bit <= mask:
        if mask & bit:
            index = index + bit - 2 * bit * lax.rem(lax.div(index, bit), 2)
        bit *= 2
    return index


def halves(x):
    high = x.astype(jnp.bfloat16)
    return high, (x - high.astype(jnp.float32)).astype(jnp.bfloat16)


def product(left, right, dims):
    def one(a, b):
        return lax.dot_general(a, b, (dims, ((), ())), preferred_element_type=jnp.float32)

    (lh, ll), (rh, rl) = left, right
    return one(lh, rh) + (one(lh, rl) + one(ll, rh))


def left_product(left, right):
    return product(halves(left), halves(right), ((0,), (0,)))


def right_product(left, right):
    return product(halves(left), right, ((1,), (0,)))


def tile_of(rows, step, most):
    count = rows // step
    best = max(k for k in range(1, most // step + 1) if count % k == 0)
    return best * step


def kernel(grid_rows, chips, matrix, leaf_v, leaf_t, tree_v, tree_t, out,
           work, vectors, inner, scaled, top, hub, other, pair_v, pair_t, node_map,
           load_sem, tree_sem, store_sem, send_sem, recv_sem, core_send, core_recv, top_send, top_recv):
    panels, own_rows, width = leaf_v.shape
    rows = work.shape[0]
    levels = grid_rows.bit_length() - 1
    bits = chips.bit_length() - 1
    half_rows = own_rows // 2
    unit = 2 * own_rows
    position = lax.axis_index("row")
    column = lax.axis_index("col")
    chip = lax.div(column, 2)
    core = lax.rem(column, 2)

    def device(which_chip, which_core):
        return {"row": position, "col": which_chip * 2 + which_core}

    def load_work(r):
        start = pl.ds(pl.multiple_of(flip(chip, r) * unit, unit), unit)
        return pltpu.make_async_copy(matrix.at[start], work.at[start], load_sem.at[panels + r])

    def load_own(p):
        start = pl.ds(pl.multiple_of(column * own_rows, own_rows), own_rows)
        return pltpu.make_async_copy(leaf_v.at[p], vectors.at[p, start], load_sem.at[p])

    def load_pair(p, level):
        node = grid_rows - (grid_rows >> level) + lax.div(position, 2 << level)
        return (pltpu.make_async_copy(tree_v.at[p, node], pair_v.at[p, level], tree_sem.at[p, level, 0]),
                pltpu.make_async_copy(tree_t.at[p, node], pair_t.at[p, level], tree_sem.at[p, level, 1]))

    load_own(0).start()
    for r in range(chips):
        load_work(r).start()
    for p in range(1, panels):
        load_own(p).start()
    for p in range(panels):
        for level in range(levels):
            for copy in load_pair(p, level):
                copy.start()

    barrier = pltpu.get_barrier_semaphore()
    partners = [device(chip, 1 - core)]
    partners += [device(flip(chip, 1 << b), core) for b in range(bits)]
    sideways = {"row": flip(position, 1), "col": column}
    across = {"row": grid_rows - 1 - position, "col": column}
    partners += [sideways, across]
    for partner in partners:
        pl.semaphore_signal(barrier, inc=1, device_id=partner, device_id_type=MESH)
    pl.semaphore_wait(barrier, len(partners))

    orders = [list(range(bits)), list(reversed(range(bits)))]

    def piece(p, r, h, on_core):
        start = (flip(chip, r) * 2 + on_core) * own_rows + h * half_rows
        return vectors.at[p, pl.ds(pl.multiple_of(start, half_rows), half_rows)]

    def source(p, r, h):
        if r == 0:
            return leaf_v.at[p, pl.ds(h * half_rows, half_rows)]
        return piece(p, r, h, core)

    def chip_copy(p, r, h, bit):
        return pltpu.make_async_remote_copy(
            source(p, r, h), piece(p, r, h, core), send_sem.at[p, r, h, bit],
            recv_sem.at[p, r | 1 << bit, h], device_id=device(flip(chip, 1 << bit), core), device_id_type=MESH)

    def core_copy(p, r, h):
        return pltpu.make_async_remote_copy(
            source(p, r, h), piece(p, r, h, core), core_send.at[p, r, h],
            core_recv.at[p, r, h], device_id=device(chip, 1 - core), device_id_type=MESH)

    def core_arrival(p, r, h):
        there = piece(p, r, h, 1 - core)
        pltpu.make_async_remote_copy(
            there, there, core_send.at[p, r, h], core_recv.at[p, r, h],
            device_id=device(chip, 1 - core), device_id_type=MESH).wait_recv()

    def chip_arrival(p, r, h):
        here = piece(p, r, h, core)
        pltpu.make_async_remote_copy(
            here, here, core_send.at[p, r, h], recv_sem.at[p, r, h],
            device_id=device(chip, 1 - core), device_id_type=MESH).wait_recv()

    started = []

    def start(copy):
        copy.start()
        started.append(copy)

    def send_own(p):
        for k in range(bits):
            for h in range(2):
                start(chip_copy(p, 0, h, orders[h][k]))
        for h in range(2):
            start(core_copy(p, 0, h))

    events = []
    for s in range(bits):
        for h in range(2):
            before = orders[h][:s]
            for m in range(chips):
                if m & ~sum(1 << b for b in before) == 0:
                    events.append((s, bin(m).count("1"), m | 1 << orders[h][s], h))
    events.sort()

    def arrive(p, event):
        s, _, r, h = event
        chip_arrival(p, r, h)
        for bit in orders[h][s + 1:]:
            start(chip_copy(p, r, h, bit))
        start(core_copy(p, r, h))

    tile = tile_of(unit, min(unit, 256), 512)

    def accumulate(p, first, count):
        for r in range(first, first + count):
            for h in range(2):
                core_arrival(p, r, h)
            if p == 0:
                load_work(r).wait()
        if first == 0:
            load_own(p).wait()

        def step(i, carry):
            r = lax.div(i, unit // tile) + first
            at = chip
            for b in range(bits):
                set_bit = lax.rem(lax.div(r, 1 << b), 2)
                have = lax.rem(lax.div(chip, 1 << b), 2)
                at = at + (1 << b) * set_bit * (1 - 2 * have)
            start_row = pl.multiple_of(at * unit + lax.rem(i, unit // tile) * tile, tile)
            inner[...] += left_product(vectors[p, pl.ds(start_row, tile)], work[pl.ds(start_row, tile)])
            return carry

        lax.fori_loop(0, count * (unit // tile), step, 0)

    down = tile_of(rows - width, width, 768)

    downs = (rows - width) // down

    def subtract(p, first, last):
        def step(i, carry):
            span = pl.ds(pl.multiple_of(width + i * down, width), down)
            work[span] = work[span] - right_product(vectors[p, span], (scaled[0], scaled[1]))
            return carry

        lax.fori_loop(first, last, step, 0)

    chunks, _, part = top.shape
    low, middle_low, middle_high = position == 0, position == 1, position == 2
    middle = jnp.logical_or(middle_low, middle_high)

    def exchange(buffer, p, j, stage, target):
        return pltpu.make_async_remote_copy(
            buffer, other.at[p, j, stage], top_send.at[p, j, stage], top_recv.at[p, j, stage],
            device_id=target, device_id_type=MESH)

    def prepare(p):
        for level in range(levels):
            for copy in load_pair(p, level):
                copy.wait()
            pair = halves(pair_v[p, level])
            weight = product(halves(pair_t[p, level]), pair, ((0,), (1,)))
            whole = right_product(pair_v[p, level], halves(weight))
            node_map[p, level, 0], node_map[p, level, 1] = halves(whole)

    def mapped(p, level, to, count, source, value):
        block = (pl.ds(to, count), pl.ds(source, width))
        return product((node_map[(p, level, 0) + block], node_map[(p, level, 1) + block]), halves(value), ((1,), (0,)))

    def head(p):
        weight = halves(left_product(leaf_t[p], inner[...]))
        scaled[0], scaled[1] = weight
        above = halves(vectors[p, :width])
        for j in range(chunks):
            columns = slice(j * part, (j + 1) * part)
            before = work[:width, columns]
            top[j] = before - product(above, (weight[0][:, columns], weight[1][:, columns]), ((1,), (0,)))

            @pl.when(jnp.logical_not(middle_low))
            def _(j=j):
                exchange(top.at[j], p, j, 0, sideways).start()

    def head_part(p, j):
        columns = slice(j * part, (j + 1) * part)
        before = top[j]
        inside = inner[:, columns] + left_product(vectors[p, :width], before)
        weight = halves(left_product(leaf_t[p], inside))
        scaled[0, :, columns], scaled[1, :, columns] = weight
        top[j] = before - right_product(vectors[p, :width], weight)

        @pl.when(jnp.logical_not(middle_low))
        def _():
            exchange(top.at[j], p, j, 0, sideways).start()

    def first_level(p, j):
        @pl.when(middle_low)
        def _():
            change = mapped(p, 0, 0, 2 * width, width, top[j])
            exchange(top.at[j], p, j, 0, sideways).wait_recv()
            theirs = other[p, j, 0]
            change = change + mapped(p, 0, 0, 2 * width, 0, theirs)
            hub[p, j] = theirs - change[:width]
            exchange(hub.at[p, j], p, j, 1, across).start()
            top[j] = top[j] - change[width:]

        @pl.when(position > 1)
        def _():
            mine = pl.multiple_of(lax.rem(position, 2) * width, width)
            theirs = pl.multiple_of(width - lax.rem(position, 2) * width, width)
            change = mapped(p, 0, mine, width, mine, top[j])
            copy = exchange(top.at[j], p, j, 0, sideways)
            copy.wait_recv()
            change = change + mapped(p, 0, mine, width, theirs, other[p, j, 0])
            copy.wait_send()
            top[j] = top[j] - change

            @pl.when(middle_high)
            def _():
                exchange(top.at[j], p, j, 1, across).start()

    def second_level(p, j):
        def update(buffer, half):
            mine, theirs = half * width, (1 - half) * width
            change = mapped(p, 1, mine, width, mine, buffer[...])
            copy = exchange(buffer, p, j, 1, across)
            copy.wait_recv()
            change = change + mapped(p, 1, mine, width, theirs, other[p, j, 1])
            copy.wait_send()
            buffer[...] = buffer[...] - change

        @pl.when(middle_low)
        def _():
            update(hub.at[p, j], 0)
            exchange(hub.at[p, j], p, j, 2, sideways).start()

        @pl.when(middle_high)
        def _():
            update(top.at[j], 1)

    def finish(p, j):
        @pl.when(low)
        def _():
            exchange(top.at[j], p, j, 0, sideways).wait_send()
            exchange(hub.at[p, j], p, j, 2, sideways).wait_recv()
            top[j] = other[p, j, 2]

    stage_one, stage_two, late = events[:-4], events[-4:-2], events[-2:]
    inner[...] = jnp.zeros_like(inner)
    send_own(0)
    accumulate(0, 0, 1)
    for p in range(panels):
        prepare(p)
    for event in stage_one + stage_two:
        arrive(0, event)
    if panels > 1:
        send_own(1)
    accumulate(0, 1, chips - 2)
    for event in late:
        arrive(0, event)
    accumulate(0, chips - 1, 1)
    head(0)
    for p in range(panels):
        q = p + 1
        if q == panels:
            subtract(p, 0, downs // 2 + 1)
            first_level(p, 0)
            first_level(p, 1)
            subtract(p, downs // 2 + 1, downs)
            span = pl.ds(width, rows - width)
            rest = pltpu.make_async_copy(work.at[span], out.at[span], store_sem.at[chunks])
            rest.start()
            for j in range(2, chunks):
                second_level(p, j - 2)
                first_level(p, j)
            for j in range(chunks - 2, chunks):
                second_level(p, j)
            last = []
            for j in range(chunks):
                finish(p, j)
                copy = pltpu.make_async_copy(
                    top.at[j], out.at[pl.ds(0, width), pl.ds(j * part, part)], store_sem.at[j])
                copy.start()
                last.append(copy)
            for copy in last:
                copy.wait()
            rest.wait()
            break
        subtract(p, 0, downs)
        work[:width] = jnp.zeros((width, work.shape[1]), jnp.float32)
        inner[...] = jnp.zeros_like(inner)
        todo = [functools.partial(arrive, q, event) for event in stage_one]
        todo += [functools.partial(first_level, p, j) for j in range(2)]
        todo += [functools.partial(accumulate, q, 0, 1)]
        todo += [functools.partial(arrive, q, event) for event in stage_two]
        if q + 1 < panels:
            todo += [functools.partial(send_own, q + 1)]
        todo += [functools.partial(first_level, p, 2), functools.partial(second_level, p, 0)]
        todo += [functools.partial(accumulate, q, 1, chips - 2)]
        todo += [functools.partial(first_level, p, 3), functools.partial(second_level, p, 1)]
        todo += [functools.partial(arrive, q, event) for event in late]
        todo += [functools.partial(second_level, p, 2), functools.partial(accumulate, q, chips - 1, 1)]
        todo += [functools.partial(second_level, p, 3)]
        for step in todo:
            step()
        for j in range(chunks):
            finish(p, j)
            head_part(q, j)
    for p in range(panels):
        for j in range(chunks):
            @pl.when(middle_low)
            def _(p=p, j=j):
                exchange(hub.at[p, j], p, j, 2, sideways).wait_send()
    for copy in started:
        copy.wait_send()


def solution(mesh):
    grid_rows = mesh.shape["row"]
    chips = mesh.shape["col"] // 2
    levels = grid_rows.bit_length() - 1
    bits = chips.bit_length() - 1

    def local(matrix, leaf_v, leaf_t, tree_v, tree_t):
        rows, columns = matrix.shape
        chunks = 4
        part = columns // chunks
        panels, _, width = leaf_v.shape
        f32, dma = jnp.float32, pltpu.SemaphoreType.DMA
        hbm = pl.BlockSpec(memory_space=pltpu.HBM)
        vmem = pl.BlockSpec(memory_space=pltpu.VMEM)
        return pl.pallas_call(
            functools.partial(kernel, grid_rows, chips),
            out_shape=jax.ShapeDtypeStruct(matrix.shape, f32),
            in_specs=[hbm, hbm, vmem, hbm, hbm],
            out_specs=pl.BlockSpec(memory_space=pl.ANY),
            scratch_shapes=[
                pltpu.VMEM((rows, columns), f32),
                pltpu.VMEM((panels, rows, width), f32),
                pltpu.VMEM((width, columns), f32),
                pltpu.VMEM((2, width, columns), jnp.bfloat16),
                pltpu.VMEM((chunks, width, part), f32),
                pltpu.VMEM((panels, chunks, width, part), f32),
                pltpu.VMEM((panels, chunks, 3, width, part), f32),
                pltpu.VMEM((panels, levels, 2 * width, width), f32),
                pltpu.VMEM((panels, levels, width, width), f32),
                pltpu.VMEM((panels, levels, 2, 2 * width, 2 * width), jnp.bfloat16),
                dma((panels + chips,)),
                dma((panels, levels, 2)),
                dma((chunks + 1,)),
                dma((panels, chips, 2, bits)),
                dma((panels, chips, 2)),
                dma((panels, chips, 2)),
                dma((panels, chips, 2)),
                dma((panels, chunks, 3)),
                dma((panels, chunks, 3)),
            ],
            compiler_params=pltpu.CompilerParams(
                collective_id=0, has_side_effects=True, vmem_limit_bytes=36 * 1024 * 1024
            ),
        )(matrix, leaf_v, leaf_t, tree_v, tree_t)

    placed = (P("row", "col"), P(None, ("row", "col"), None), P(None, "row", None), P(), P())
    return jax.shard_map(local, mesh=mesh, in_specs=placed, out_specs=P("row", "col"), check_vma=False)
```
